32 devices in a mesh: gz: 4 (over y, x), phi: 8 (over z, core).
Axes of the slice: x: 2, y: 2, z: 4, core: 2. Of those that a mesh axis runs over, the one named last changes fastest.
Arguments:
- potential_in: float32 [256, 512, 256], P('phi', 'gz'), may hold values from -6 to 6
- charge: float32 [256, 512, 256], P('phi', 'gz'), may hold values from -6 to 6
- cell_kind: int32 [256, 512, 256], P('phi', 'gz'), may hold values from 0 to 2, as said below
Outputs:
- potential: float32 [256, 512, 256], P('phi', 'gz')
- shift_r: float32 [256, 512, 256], P('phi', 'gz')
- shift_rphi: float32 [256, 512, 256], P('phi', 'gz')
The draws below stay inside these ranges and needn't reach their ends.
Inputs may be any that keep to these rules, and one draw needn't show every extreme that they name: `cell_kind`: 0 marks a free cell, 1 an electrode cell held at zero potential, 2 a boundary cell held at its given potential.
All inputs are finite; a program needn't handle non-finite values.
Results may differ from the reference program's by a relative error of at most 0.000073.
Values sent between devices are 32-bit elements; how exact they have to be, the bound alone decides.
A program may use at most 128 MiB of HBM per device.

```python
import math
import jax
import jax.numpy as jnp

NR = 256
PASSES = 3
NPHI = 256
NZ = 512


def draw_cell_kind(key, part):
    values = jax.random.randint(jax.random.fold_in(key, 17), (NPHI, NZ, NR), 0, 16)
    return jnp.where(values == 0, 1, jnp.where(values == 1, 2, 0)).astype(jnp.int32)


def levels(own_key, shape, split, least, top_value):
    factor_of = 1.0
    for position, blocks in split:
        draws = jax.random.uniform(jax.random.fold_in(jax.random.fold_in(own_key, 6), position), (blocks,), jnp.float32, least / len(split), top_value / len(split))
        factor_of = factor_of * jnp.repeat(jnp.exp(draws), shape[position] // blocks).reshape((-1,) + (1,) * (len(shape) - 1 - position))
    return factor_of


def gaussian(key, extent, deviation, bound, split=(), held_as=jnp.bfloat16):
    level = levels(key, extent, split, -0.22, 0.18) if split else 1.0
    result = jax.random.normal(key, extent, jnp.float32) * deviation * level
    return jnp.minimum(jnp.maximum(result, -bound), bound).astype(held_as)


def setup_inputs(seed: int = 0) -> dict:
    splits = jax.random.split(jax.random.key(seed), 4)
    return {
        "potential_in": gaussian(splits[0], (NPHI, NZ, NR), 1.0, 6.0, ((0, 8), (1, 4)), jnp.float32),
        "charge": gaussian(splits[1], (NPHI, NZ, NR), 1.0, 6.0, ((0, 8), (1, 4)), jnp.float32),
        "cell_kind": draw_cell_kind(jax.random.fold_in(splits[3], 71), 0),
    }


relax_weight = 1.5


def coefficients(radial, sectors):
    radius = radial * 0.5 + jnp.arange(radial, dtype=jnp.float32) + 0.5
    step_phi = 2.0 * math.pi / sectors
    outward = 1.0 + 0.5 / radius
    inward = 1.0 - 0.5 / radius
    beside_all = 1.0 / (radius * step_phi) ** 2
    diag = 4.0 + 2.0 * beside_all
    return radius, step_phi, outward, inward, beside_all, diag


def radial_next(field):
    return jnp.concatenate([field[:, :, 1:], jnp.zeros_like(field[:, :, :1])], 2)


def radial_prev(field):
    return jnp.concatenate([jnp.zeros_like(field[:, :, :1]), field[:, :, :-1]], 2)


def reference(potential_in, charge, cell_kind):
    sectors, depth, radial = potential_in.shape
    radius, step_phi, outward, inward, beside_all, diag = coefficients(radial, sectors)
    parity = (jnp.arange(sectors, dtype=jnp.int32)[:, None, None] + jnp.arange(depth, dtype=jnp.int32)[None, :, None] + jnp.arange(radial, dtype=jnp.int32)[None, None, :]) % 2
    free = cell_kind == 0
    field = jnp.where(cell_kind == 1, jnp.zeros_like(potential_in), potential_in)
    for sweep in range(PASSES):
        for color in (0, 1):
            next_z = jnp.concatenate([field[:, 1:], jnp.zeros_like(field[:, :1])], 1)
            prev_z = jnp.concatenate([jnp.zeros_like(field[:, :1]), field[:, :-1]], 1)
            total = outward * radial_next(field) + inward * radial_prev(field) + beside_all * (jnp.roll(field, -1, 0) + jnp.roll(field, 1, 0)) + next_z + prev_z
            target = (total + charge) / diag
            update = jnp.logical_and(parity == color, free)
            field = jnp.where(update, field + relax_weight * (target - field), field)
    field_r = -0.5 * (radial_next(field) - radial_prev(field))
    field_phi = -0.5 * (jnp.roll(field, -1, 0) - jnp.roll(field, 1, 0)) / (radius * step_phi)
    drift_r = (field_r + 0.3 * field_phi) / (1.09 * 32.0)
    drift_phi = (field_phi - 0.3 * field_r) / (1.09 * 32.0)
    shift_r = jnp.flip(jnp.cumsum(jnp.flip(drift_r, 1), 1), 1)
    shift_rphi = jnp.flip(jnp.cumsum(jnp.flip(drift_phi, 1), 1), 1)
    return field, shift_r, shift_rphi
```

```python
import functools
import math

import jax
import jax.numpy as jnp
import numpy as np
from jax import lax
from jax.experimental import pallas as pl
from jax.experimental.pallas import tpu as pltpu
from jax.sharding import PartitionSpec as P

PASSES = 3
HALVES = 2 * PASSES
RELAX = 1.5
FIXED = 1e30
MESH = pl.DeviceIdType.MESH
PAD = 8
LOAD_PAIRS = 2


def parity_mask(radial):
    row = lax.broadcasted_iota(jnp.int32, (8, radial), 0)
    lane = lax.broadcasted_iota(jnp.int32, (8, radial), 1)
    return (row + lane) % 2 == 0


def relax_kernel(
    slabs, rings, pot, chg, kind, coef, field, carry,
    pot_in, chg_in, kind_in, source, jsend, jrecv, zsend, zrecv, total, total_recv,
    load_sem, jsend_sem, jrecv_sem, zsend_sem, zrecv_sem, tsend_sem, trecv_sem,
):
    pairs = source.shape[1]
    depth = source.shape[2]
    radial = source.shape[3]
    half = depth // 2
    slab = lax.axis_index("gz")
    ring = lax.axis_index("phi")
    right, left = lax.rem(ring + 1, rings), lax.rem(ring + rings - 1, rings)

    chunks = [(0, 1), (pairs - 1, 1)]
    at = 1
    while at < pairs - 1:
        chunks.append((at, min(LOAD_PAIRS, pairs - 1 - at)))
        at += LOAD_PAIRS

    def loads(index):
        first, count = chunks[index]
        part = pl.ds(2 * first, 2 * count)
        return [
            pltpu.make_async_copy(src.at[part], dst.at[part], load_sem.at[index, n])
            for n, (src, dst) in enumerate(((pot, pot_in), (chg, chg_in), (kind, kind_in)))
        ]

    for index in range(len(chunks)):
        for copy in loads(index):
            copy.start()

    barrier = pltpu.get_barrier_semaphore()
    for neighbour in (left, right):
        pl.semaphore_signal(barrier, inc=1, device_id={"phi": neighbour}, device_id_type=MESH)
    for step in range(1, slabs):
        peer = lax.rem(slab + step, slabs)
        pl.semaphore_signal(barrier, inc=1, device_id={"gz": peer}, device_id_type=MESH)

    def prepare(pair):
        mask = parity_mask(radial)
        weight = coef[3]
        for row in range(0, depth, 8):
            rows = pl.ds(row, 8)
            out = pl.ds(row + PAD, 8)
            plane, charges = [], []
            for side in range(2):
                what = kind_in[2 * pair + side, rows, :]
                plane.append(jnp.where(what == 1, 0.0, pot_in[2 * pair + side, rows, :]))
                charges.append(
                    jnp.where(what == 0, weight * chg_in[2 * pair + side, rows, :], FIXED)
                )
            field[0, pair + 1, out, :] = jnp.where(mask, plane[0], plane[1])
            field[1, pair + 1, out, :] = jnp.where(mask, plane[1], plane[0])
            source[0, pair, rows, :] = jnp.where(mask, charges[0], charges[1])
            source[1, pair, rows, :] = jnp.where(mask, charges[1], charges[0])

    def jcopy(turn, side):
        return pltpu.make_async_remote_copy(
            src_ref=jsend.at[turn, side],
            dst_ref=jrecv.at[turn, side],
            send_sem=jsend_sem.at[turn, side],
            recv_sem=jrecv_sem.at[turn, side],
            device_id={"phi": (right, left)[side]},
            device_id_type=MESH,
        )

    def zcopy(turn, side):
        return pltpu.make_async_remote_copy(
            src_ref=zsend.at[turn, side],
            dst_ref=zrecv.at[turn, side],
            send_sem=zsend_sem.at[turn, side],
            recv_sem=zrecv_sem.at[turn, side],
            device_id={"gz": (lax.rem(slab + 1, slabs), lax.rem(slab + slabs - 1, slabs))[side]},
            device_id_type=MESH,
        )

    has_next, has_prev = slab < slabs - 1, slab > 0

    def send_j(turn, color, side):
        pair = (pairs, 1)[side]
        mask = parity_mask(radial)
        first = (color == 1) == (side == 0)
        for row in range(0, half, 8):
            upper = field[color, pair, pl.ds(PAD + row, 8), :]
            lower = pltpu.roll(field[color, pair, pl.ds(PAD + row + half, 8), :], 1, axis=1)
            jsend[turn, side, pl.ds(row, 8), :] = (
                jnp.where(mask, upper, lower) if first else jnp.where(mask, lower, upper)
            )
        jcopy(turn, side).start()

    def take_j(turn, color, side):
        jcopy(turn, side).wait_recv()
        pair = (0, pairs + 1)[side]
        for row in range(0, half, 8):
            face = jrecv[turn, side, pl.ds(row, 8), :]
            field[color, pair, pl.ds(PAD + row, 8), :] = face
            field[color, pair, pl.ds(PAD + row + half, 8), :] = pltpu.roll(face, radial - 1, axis=1)

    def send_z(turn, color):
        for pair in range(pairs):
            zsend[turn, 0, pair] = field[color, pair + 1, pl.ds(PAD + depth - 1, 1), :]
            zsend[turn, 1, pair] = field[color, pair + 1, pl.ds(PAD, 1), :]

        @pl.when(has_next)
        def _():
            zcopy(turn, 0).start()

        @pl.when(has_prev)
        def _():
            zcopy(turn, 1).start()

    def take_z(turn, color):
        @pl.when(has_prev)
        def _():
            zcopy(turn, 0).wait_recv()
            for pair in range(pairs):
                field[color, pair + 1, pl.ds(PAD - 1, 1), :] = zrecv[turn, 0, pair]

        @pl.when(has_next)
        def _():
            zcopy(turn, 1).wait_recv()
            for pair in range(pairs):
                field[color, pair + 1, pl.ds(PAD + depth, 1), :] = zrecv[turn, 1, pair]

    def update(pair, color):
        other = 1 - color
        mask = parity_mask(radial)
        out_c, in_c, around_c, z_c = coef[0], coef[1], coef[2], coef[3]
        before, after = (pair - 1, pair + 1) if color == 0 else (pair + 1, pair - 1)
        for row in range(0, depth, 8):
            rows = pl.ds(row + PAD, 8)
            own = field[color, pair, rows, :]
            near = field[other, pair, rows, :]
            beside = near + jnp.where(mask, field[other, before, rows, :], field[other, after, rows, :])
            along = (
                field[other, pair, pl.ds(row + PAD - 1, 8), :]
                + field[other, pair, pl.ds(row + PAD + 1, 8), :]
            )
            put = source[color, pair - 1, pl.ds(row, 8), :]
            fresh = (
                put
                - (RELAX - 1.0) * own
                + out_c * pltpu.roll(near, radial - 1, axis=1)
                + in_c * pltpu.roll(near, 1, axis=1)
                + around_c * beside
                + z_c * along
            )
            field[color, pair, rows, :] = jnp.where(put < 0.5 * FIXED, fresh, own)

    edge = jnp.zeros((PAD, radial), jnp.float32)
    for color in range(2):
        for pair in range(1, pairs + 1):
            field[color, pair, pl.ds(0, PAD), :] = edge
            field[color, pair, pl.ds(PAD + depth, PAD), :] = edge

    for index in range(2):
        for copy in loads(index):
            copy.wait()
        prepare(chunks[index][0])
    pl.semaphore_wait(barrier, 2 + slabs - 1)
    for side in range(2):
        send_j(0, 1, side)
    for index in range(2, len(chunks)):
        for copy in loads(index):
            copy.wait()
        first, count = chunks[index]
        lax.fori_loop(first, first + count, lambda a, _: (prepare(a), 0)[1], 0)
    send_z(0, 1)

    for turn in range(HALVES):
        color = turn % 2
        take_z(turn, 1 - color)
        for side in range(2):
            take_j(turn, 1 - color, side)
        for side in range(2):
            update((pairs, 1)[side], color)
            send_j(turn + 1, color, side)
        lax.fori_loop(2, pairs, lambda a, _: (update(a, color), 0)[1], 0)
        if turn + 1 < HALVES:
            send_z(turn + 1, color)

    def sum_up(pair):
        mask = parity_mask(radial)
        even = jnp.zeros((8, radial), jnp.float32)
        odd = jnp.zeros((8, radial), jnp.float32)
        for row in range(0, depth, 8):
            red = field[0, pair, pl.ds(row + PAD, 8), :]
            black = field[1, pair, pl.ds(row + PAD, 8), :]
            even += jnp.where(mask, red, black)
            odd += jnp.where(mask, black, red)
        total[pair, pl.ds(0, 1), :] = jnp.sum(even, axis=0, keepdims=True)
        total[pair, pl.ds(1, 1), :] = jnp.sum(odd, axis=0, keepdims=True)

    lax.fori_loop(1, pairs + 1, lambda a, _: (sum_up(a), 0)[1], 0)
    for side in range(2):
        take_j(HALVES, 1, side)
    sum_up(0)
    sum_up(pairs + 1)

    def tcopy(step):
        return pltpu.make_async_remote_copy(
            src_ref=total,
            dst_ref=total_recv.at[step - 1],
            send_sem=tsend_sem.at[step - 1],
            recv_sem=trecv_sem.at[step - 1],
            device_id={"gz": lax.rem(slab + step, slabs)},
            device_id_type=MESH,
        )

    for step in range(1, slabs):
        tcopy(step).start()
    beyond = jnp.zeros(carry.shape, jnp.float32)
    for step in range(1, slabs):
        tcopy(step).wait_recv()
        beyond = beyond + jnp.where(step > slab, total_recv[step - 1], 0.0)
    carry[...] = beyond

    for step in range(1, slabs):
        tcopy(step).wait_send()
    for turn in range(HALVES + 1):
        for side in range(2):
            jcopy(turn, side).wait_send()
    for turn in range(HALVES):
        @pl.when(has_next)
        def _():
            zcopy(turn, 0).wait_send()

        @pl.when(has_prev)
        def _():
            zcopy(turn, 1).wait_send()


def drift_kernel(coef, field, carry, potential, shift_r, shift_phi, sums):
    step = pl.program_id(0)
    depth, radial = potential.shape[1], potential.shape[2]
    mask = parity_mask(radial)
    row = lax.broadcasted_iota(jnp.int32, (8, radial), 0)
    slot = lax.rem(step, 3)
    for side in range(2):
        run = jnp.broadcast_to(carry[0, pl.ds(side, 1), :], (8, radial))
        for at in range(depth - 8, -8, -8):
            red = field[0, 0, pl.ds(at + PAD, 8), :]
            black = field[1, 0, pl.ds(at + PAD, 8), :]
            part = jnp.where(mask, red, black) if side == 0 else jnp.where(mask, black, red)
            for hop in (1, 2, 4):
                part = part + jnp.where(row < 8 - hop, pltpu.roll(part, 8 - hop, axis=0), 0.0)
            part = part + run
            sums[slot, side, pl.ds(at, 8), :] = part
            run = jnp.broadcast_to(part[0:1, :], (8, radial))

    @pl.when(step >= 2)
    def _():
        mid, low = lax.rem(step + 2, 3), lax.rem(step + 1, 3)
        out_c, in_c, phi_c = coef[4], coef[5], coef[6]
        for at in range(0, depth, 8):
            rows = pl.ds(at, 8)
            planes = (sums[low, 1, rows, :], sums[mid, 0, rows, :], sums[mid, 1, rows, :], sums[slot, 0, rows, :])
            for side in range(2):
                here = planes[side + 1]
                along_r = out_c * pltpu.roll(here, radial - 1, axis=1) + in_c * pltpu.roll(here, 1, axis=1)
                along_phi = phi_c * (planes[side + 2] - planes[side])
                shift_r[side, rows, :] = along_r + 0.3 * along_phi
                shift_phi[side, rows, :] = along_phi - 0.3 * along_r


def coefficients(radial, sectors):
    radius = radial * 0.5 + np.arange(radial, dtype=np.float64) + 0.5
    step_phi = 2.0 * math.pi / sectors
    around = 1.0 / (radius * step_phi) ** 2
    diag = 4.0 + 2.0 * around
    has_next = np.arange(radial) < radial - 1
    has_prev = np.arange(radial) > 0
    drift = 1.0 / (1.09 * 32.0)
    rows = [
        RELAX * (1.0 + 0.5 / radius) / diag * has_next,
        RELAX * (1.0 - 0.5 / radius) / diag * has_prev,
        RELAX * around / diag,
        RELAX / diag,
        -0.5 * drift * has_next,
        0.5 * drift * has_prev,
        -0.5 * drift / (radius * step_phi),
        np.zeros(radial),
    ]
    stacked = np.stack(rows).astype(np.float32)
    return jnp.asarray(np.ascontiguousarray(np.broadcast_to(stacked[:, None, :], (8, 8, radial))))


def local(slabs, rings, potential_in, charge, cell_kind):
    sectors, depth, radial = potential_in.shape
    pairs = sectors // 2
    tall = depth + 2 * PAD
    coef = coefficients(radial, sectors * rings)
    any_spec = pl.BlockSpec(memory_space=pl.ANY)
    vmem_spec = pl.BlockSpec(memory_space=pltpu.VMEM)
    chunks = 2 + -(-(pairs - 2) // LOAD_PAIRS)
    f32 = jnp.float32
    field, carry = pl.pallas_call(
        functools.partial(relax_kernel, slabs, rings),
        out_shape=(
            jax.ShapeDtypeStruct((2, pairs + 2, tall, radial), f32),
            jax.ShapeDtypeStruct((pairs + 2, 2, radial), f32),
        ),
        in_specs=[any_spec, any_spec, any_spec, vmem_spec],
        out_specs=(vmem_spec, vmem_spec),
        scratch_shapes=[
            pltpu.VMEM((sectors, depth, radial), f32),
            pltpu.VMEM((sectors, depth, radial), f32),
            pltpu.VMEM((sectors, depth, radial), jnp.int32),
            pltpu.VMEM((2, pairs, depth, radial), f32),
            pltpu.VMEM((HALVES + 1, 2, depth // 2, radial), f32),
            pltpu.VMEM((HALVES + 1, 2, depth // 2, radial), f32),
            pltpu.VMEM((HALVES, 2, pairs, 1, radial), f32),
            pltpu.VMEM((HALVES, 2, pairs, 1, radial), f32),
            pltpu.VMEM((pairs + 2, 2, radial), f32),
            pltpu.VMEM((slabs - 1, pairs + 2, 2, radial), f32),
            pltpu.SemaphoreType.DMA((chunks, 3)),
            pltpu.SemaphoreType.DMA((HALVES + 1, 2)),
            pltpu.SemaphoreType.DMA((HALVES + 1, 2)),
            pltpu.SemaphoreType.DMA((HALVES, 2)),
            pltpu.SemaphoreType.DMA((HALVES, 2)),
            pltpu.SemaphoreType.DMA((slabs - 1,)),
            pltpu.SemaphoreType.DMA((slabs - 1,)),
        ],
        compiler_params=pltpu.CompilerParams(collective_id=0, has_side_effects=True),
    )(potential_in, charge, cell_kind, coef)

    block = jax.ShapeDtypeStruct((sectors, depth, radial), f32)

    def out_map(g):
        return (jnp.maximum(g - 2, 0), 0, 0)

    return pl.pallas_call(
        drift_body,
        out_shape=(block, block, block),
        grid=(pairs + 2,),
        in_specs=[
            pl.BlockSpec((8, 8, radial), lambda g: (0, 0, 0)),
            pl.BlockSpec((2, 1, tall, radial), lambda g: (0, g, 0, 0)),
            pl.BlockSpec((1, 2, radial), lambda g: (g, 0, 0)),
        ],
        out_specs=(pl.BlockSpec((2, depth, radial), lambda g: (jnp.clip(g - 1, 0, pairs - 1), 0, 0)),)
        + (pl.BlockSpec((2, depth, radial), out_map),) * 2,
        scratch_shapes=[pltpu.VMEM((3, 2, depth, radial), f32)],
    )(coef, field, carry)


def drift_body(coef, field, carry, potential, shift_r, shift_phi, sums):
    step = pl.program_id(0)
    depth, radial = potential.shape[1], potential.shape[2]

    @pl.when(jnp.logical_and(step >= 1, step < pl.num_programs(0) - 1))
    def _():
        mask = parity_mask(radial)
        for at in range(0, depth, 8):
            red = field[0, 0, pl.ds(at + PAD, 8), :]
            black = field[1, 0, pl.ds(at + PAD, 8), :]
            potential[0, pl.ds(at, 8), :] = jnp.where(mask, red, black)
            potential[1, pl.ds(at, 8), :] = jnp.where(mask, black, red)

    drift_kernel(coef, field, carry, potential, shift_r, shift_phi, sums)


def solution(mesh):
    spec = P("phi", "gz", None)
    body = functools.partial(local, mesh.shape["gz"], mesh.shape["phi"])
    return jax.shard_map(body, mesh=mesh, in_specs=(spec,) * 3, out_specs=(spec,) * 3, check_vma=False)
```

```python
import functools
import math

import jax
import jax.numpy as jnp
import numpy as np
from jax import lax
from jax.experimental import pallas as pl
from jax.experimental.pallas import tpu as pltpu
from jax.sharding import PartitionSpec as P

PASSES = 3
HALVES = 2 * PASSES
RELAX = 1.5
FIXED = 1e30
MESH = pl.DeviceIdType.MESH
PAD = 8
LOAD_PAIRS = 2


def parity_mask(radial):
    row = lax.broadcasted_iota(jnp.int32, (8, radial), 0)
    lane = lax.broadcasted_iota(jnp.int32, (8, radial), 1)
    return (row + lane) % 2 == 0


def relax_kernel(
    slabs, rings, pot, chg, kind, coef, field, carry,
    pot_in, chg_in, kind_in, source, jsend, jrecv, zsend, zrecv, total, total_recv,
    load_sem, jsend_sem, jrecv_sem, zsend_sem, zrecv_sem, tsend_sem, trecv_sem,
):
    pairs = source.shape[1]
    depth = source.shape[2]
    radial = source.shape[3]
    half = depth // 2
    slab = lax.axis_index("gz")
    ring = lax.axis_index("phi")
    right, left = lax.rem(ring + 1, rings), lax.rem(ring + rings - 1, rings)

    chunks = [(0, 1), (pairs - 1, 1)]
    at = 1
    while at < pairs - 1:
        chunks.append((at, min(LOAD_PAIRS, pairs - 1 - at)))
        at += LOAD_PAIRS

    def loads(index):
        first, count = chunks[index]
        part = pl.ds(2 * first, 2 * count)
        return [
            pltpu.make_async_copy(src.at[part], dst.at[part], load_sem.at[index, n])
            for n, (src, dst) in enumerate(((pot, pot_in), (chg, chg_in), (kind, kind_in)))
        ]

    for index in range(len(chunks)):
        for copy in loads(index):
            copy.start()

    barrier = pltpu.get_barrier_semaphore()
    for neighbour in (left, right):
        pl.semaphore_signal(barrier, inc=1, device_id={"phi": neighbour}, device_id_type=MESH)
    for step in range(1, slabs):
        peer = lax.rem(slab + step, slabs)
        pl.semaphore_signal(barrier, inc=1, device_id={"gz": peer}, device_id_type=MESH)

    def prepare(pair):
        mask = parity_mask(radial)
        weight = coef[3]
        for row in range(0, depth, 8):
            rows = pl.ds(row, 8)
            out = pl.ds(row + PAD, 8)
            plane, charges = [], []
            for side in range(2):
                what = kind_in[2 * pair + side, rows, :]
                plane.append(jnp.where(what == 1, 0.0, pot_in[2 * pair + side, rows, :]))
                charges.append(
                    jnp.where(what == 0, weight * chg_in[2 * pair + side, rows, :], FIXED)
                )
            field[0, pair + 1, out, :] = jnp.where(mask, plane[0], plane[1])
            field[1, pair + 1, out, :] = jnp.where(mask, plane[1], plane[0])
            source[0, pair, rows, :] = jnp.where(mask, charges[0], charges[1])
            source[1, pair, rows, :] = jnp.where(mask, charges[1], charges[0])

    def jcopy(turn, side):
        return pltpu.make_async_remote_copy(
            src_ref=jsend.at[turn, side],
            dst_ref=jrecv.at[turn, side],
            send_sem=jsend_sem.at[turn, side],
            recv_sem=jrecv_sem.at[turn, side],
            device_id={"phi": (right, left)[side]},
            device_id_type=MESH,
        )

    def zcopy(turn, side):
        return pltpu.make_async_remote_copy(
            src_ref=zsend.at[turn, side],
            dst_ref=zrecv.at[turn, side],
            send_sem=zsend_sem.at[turn, side],
            recv_sem=zrecv_sem.at[turn, side],
            device_id={"gz": (lax.rem(slab + 1, slabs), lax.rem(slab + slabs - 1, slabs))[side]},
            device_id_type=MESH,
        )

    has_next, has_prev = slab < slabs - 1, slab > 0

    def send_j(turn, color, side):
        pair = (pairs, 1)[side]
        mask = parity_mask(radial)
        first = (color == 1) == (side == 0)
        for row in range(0, half, 8):
            upper = field[color, pair, pl.ds(PAD + row, 8), :]
            lower = pltpu.roll(field[color, pair, pl.ds(PAD + row + half, 8), :], 1, axis=1)
            jsend[turn, side, pl.ds(row, 8), :] = (
                jnp.where(mask, upper, lower) if first else jnp.where(mask, lower, upper)
            )
        jcopy(turn, side).start()

    def take_j(turn, color, side):
        jcopy(turn, side).wait_recv()
        pair = (0, pairs + 1)[side]
        for row in range(0, half, 8):
            face = jrecv[turn, side, pl.ds(row, 8), :]
            field[color, pair, pl.ds(PAD + row, 8), :] = face
            field[color, pair, pl.ds(PAD + row + half, 8), :] = pltpu.roll(face, radial - 1, axis=1)

    def send_z(turn, color):
        for pair in range(pairs):
            zsend[turn, 0, pair] = field[color, pair + 1, pl.ds(PAD + depth - 1, 1), :]
            zsend[turn, 1, pair] = field[color, pair + 1, pl.ds(PAD, 1), :]

        @pl.when(has_next)
        def _():
            zcopy(turn, 0).start()

        @pl.when(has_prev)
        def _():
            zcopy(turn, 1).start()

    def take_z(turn, color):
        @pl.when(has_prev)
        def _():
            zcopy(turn, 0).wait_recv()
            for pair in range(pairs):
                field[color, pair + 1, pl.ds(PAD - 1, 1), :] = zrecv[turn, 0, pair]

        @pl.when(has_next)
        def _():
            zcopy(turn, 1).wait_recv()
            for pair in range(pairs):
                field[color, pair + 1, pl.ds(PAD + depth, 1), :] = zrecv[turn, 1, pair]

    def update(pair, color, blocks):
        other = 1 - color
        mask = parity_mask(radial)
        out_c, in_c, around_c, z_c = coef[0], coef[1], coef[2], coef[3]
        before, after = (pair - 1, pair + 1) if color == 0 else (pair + 1, pair - 1)
        for row in blocks:
            rows = pl.ds(row + PAD, 8)
            own = field[color, pair, rows, :]
            near = field[other, pair, rows, :]
            beside = near + jnp.where(mask, field[other, before, rows, :], field[other, after, rows, :])
            along = (
                field[other, pair, pl.ds(row + PAD - 1, 8), :]
                + field[other, pair, pl.ds(row + PAD + 1, 8), :]
            )
            put = source[color, pair - 1, pl.ds(row, 8), :]
            fresh = (
                put
                - (RELAX - 1.0) * own
                + out_c * pltpu.roll(near, radial - 1, axis=1)
                + in_c * pltpu.roll(near, 1, axis=1)
                + around_c * beside
                + z_c * along
            )
            field[color, pair, rows, :] = jnp.where(put < 0.5 * FIXED, fresh, own)

    edge = jnp.zeros((PAD, radial), jnp.float32)
    for color in range(2):
        for pair in range(1, pairs + 1):
            field[color, pair, pl.ds(0, PAD), :] = edge
            field[color, pair, pl.ds(PAD + depth, PAD), :] = edge

    for index in range(2):
        for copy in loads(index):
            copy.wait()
        prepare(chunks[index][0])
    pl.semaphore_wait(barrier, 2 + slabs - 1)
    for side in range(2):
        send_j(0, 1, side)
    for index in range(2, len(chunks)):
        for copy in loads(index):
            copy.wait()
        first, count = chunks[index]
        lax.fori_loop(first, first + count, lambda a, _: (prepare(a), 0)[1], 0)
    send_z(0, 1)

    whole, ends, inner = range(0, depth, 8), (0, depth - 8), range(8, depth - 8, 8)
    for turn in range(HALVES):
        color = turn % 2
        take_z(turn, 1 - color)
        for side in range(2):
            take_j(turn, 1 - color, side)
            update((1, pairs)[side], color, whole)
            send_j(turn + 1, color, 1 - side)
        if turn + 1 < HALVES:
            lax.fori_loop(2, pairs, lambda a, _: (update(a, color, ends), 0)[1], 0)
            send_z(turn + 1, color)
            lax.fori_loop(2, pairs, lambda a, _: (update(a, color, inner), 0)[1], 0)
        else:
            lax.fori_loop(2, pairs, lambda a, _: (update(a, color, whole), 0)[1], 0)

    def sum_up(pair):
        mask = parity_mask(radial)
        even = jnp.zeros((8, radial), jnp.float32)
        odd = jnp.zeros((8, radial), jnp.float32)
        for row in range(0, depth, 8):
            red = field[0, pair, pl.ds(row + PAD, 8), :]
            black = field[1, pair, pl.ds(row + PAD, 8), :]
            even += jnp.where(mask, red, black)
            odd += jnp.where(mask, black, red)
        total[pair, pl.ds(0, 1), :] = jnp.sum(even, axis=0, keepdims=True)
        total[pair, pl.ds(1, 1), :] = jnp.sum(odd, axis=0, keepdims=True)

    lax.fori_loop(1, pairs + 1, lambda a, _: (sum_up(a), 0)[1], 0)
    for side in range(2):
        take_j(HALVES, 1, side)
    sum_up(0)
    sum_up(pairs + 1)

    def tcopy(step):
        return pltpu.make_async_remote_copy(
            src_ref=total,
            dst_ref=total_recv.at[step - 1],
            send_sem=tsend_sem.at[step - 1],
            recv_sem=trecv_sem.at[step - 1],
            device_id={"gz": lax.rem(slab + step, slabs)},
            device_id_type=MESH,
        )

    for step in range(1, slabs):
        tcopy(step).start()
    beyond = jnp.zeros(carry.shape, jnp.float32)
    for step in range(1, slabs):
        tcopy(step).wait_recv()
        beyond = beyond + jnp.where(step > slab, total_recv[step - 1], 0.0)
    carry[...] = beyond

    for step in range(1, slabs):
        tcopy(step).wait_send()
    for turn in range(HALVES + 1):
        for side in range(2):
            jcopy(turn, side).wait_send()
    for turn in range(HALVES):
        @pl.when(has_next)
        def _():
            zcopy(turn, 0).wait_send()

        @pl.when(has_prev)
        def _():
            zcopy(turn, 1).wait_send()


def drift_kernel(coef, field, carry, potential, shift_r, shift_phi, sums):
    step = pl.program_id(0)
    depth, radial = potential.shape[1], potential.shape[2]
    mask = parity_mask(radial)
    row = lax.broadcasted_iota(jnp.int32, (8, radial), 0)
    slot = lax.rem(step, 3)
    runs = [jnp.broadcast_to(carry[0, pl.ds(side, 1), :], (8, radial)) for side in range(2)]
    for at in range(depth - 8, -8, -8):
        red = field[0, 0, pl.ds(at + PAD, 8), :]
        black = field[1, 0, pl.ds(at + PAD, 8), :]
        for side in range(2):
            part = jnp.where(mask, red, black) if side == 0 else jnp.where(mask, black, red)
            for hop in (1, 2, 4):
                part = part + jnp.where(row < 8 - hop, pltpu.roll(part, 8 - hop, axis=0), 0.0)
            sums[slot, side, pl.ds(at, 8), :] = part + runs[side]
            runs[side] = runs[side] + jnp.broadcast_to(part[0:1, :], (8, radial))

    @pl.when(step >= 2)
    def _():
        mid, low = lax.rem(step + 2, 3), lax.rem(step + 1, 3)
        out_c, in_c, phi_c = coef[4], coef[5], coef[6]
        for at in range(0, depth, 8):
            rows = pl.ds(at, 8)
            planes = (sums[low, 1, rows, :], sums[mid, 0, rows, :], sums[mid, 1, rows, :], sums[slot, 0, rows, :])
            for side in range(2):
                here = planes[side + 1]
                along_r = out_c * pltpu.roll(here, radial - 1, axis=1) + in_c * pltpu.roll(here, 1, axis=1)
                along_phi = phi_c * (planes[side + 2] - planes[side])
                shift_r[side, rows, :] = along_r + 0.3 * along_phi
                shift_phi[side, rows, :] = along_phi - 0.3 * along_r


def coefficients(radial, sectors):
    radius = radial * 0.5 + np.arange(radial, dtype=np.float64) + 0.5
    step_phi = 2.0 * math.pi / sectors
    around = 1.0 / (radius * step_phi) ** 2
    diag = 4.0 + 2.0 * around
    has_next = np.arange(radial) < radial - 1
    has_prev = np.arange(radial) > 0
    drift = 1.0 / (1.09 * 32.0)
    rows = [
        RELAX * (1.0 + 0.5 / radius) / diag * has_next,
        RELAX * (1.0 - 0.5 / radius) / diag * has_prev,
        RELAX * around / diag,
        RELAX / diag,
        -0.5 * drift * has_next,
        0.5 * drift * has_prev,
        -0.5 * drift / (radius * step_phi),
        np.zeros(radial),
    ]
    stacked = np.stack(rows).astype(np.float32)
    return jnp.asarray(np.ascontiguousarray(np.broadcast_to(stacked[:, None, :], (8, 8, radial))))


def local(slabs, rings, potential_in, charge, cell_kind):
    sectors, depth, radial = potential_in.shape
    pairs = sectors // 2
    tall = depth + 2 * PAD
    coef = coefficients(radial, sectors * rings)
    any_spec = pl.BlockSpec(memory_space=pl.ANY)
    vmem_spec = pl.BlockSpec(memory_space=pltpu.VMEM)
    chunks = 2 + -(-(pairs - 2) // LOAD_PAIRS)
    f32 = jnp.float32
    field, carry = pl.pallas_call(
        functools.partial(relax_kernel, slabs, rings),
        out_shape=(
            jax.ShapeDtypeStruct((2, pairs + 2, tall, radial), f32),
            jax.ShapeDtypeStruct((pairs + 2, 2, radial), f32),
        ),
        in_specs=[any_spec, any_spec, any_spec, vmem_spec],
        out_specs=(vmem_spec, vmem_spec),
        scratch_shapes=[
            pltpu.VMEM((sectors, depth, radial), f32),
            pltpu.VMEM((sectors, depth, radial), f32),
            pltpu.VMEM((sectors, depth, radial), jnp.int32),
            pltpu.VMEM((2, pairs, depth, radial), f32),
            pltpu.VMEM((HALVES + 1, 2, depth // 2, radial), f32),
            pltpu.VMEM((HALVES + 1, 2, depth // 2, radial), f32),
            pltpu.VMEM((HALVES, 2, pairs, 1, radial), f32),
            pltpu.VMEM((HALVES, 2, pairs, 1, radial), f32),
            pltpu.VMEM((pairs + 2, 2, radial), f32),
            pltpu.VMEM((slabs - 1, pairs + 2, 2, radial), f32),
            pltpu.SemaphoreType.DMA((chunks, 3)),
            pltpu.SemaphoreType.DMA((HALVES + 1, 2)),
            pltpu.SemaphoreType.DMA((HALVES + 1, 2)),
            pltpu.SemaphoreType.DMA((HALVES, 2)),
            pltpu.SemaphoreType.DMA((HALVES, 2)),
            pltpu.SemaphoreType.DMA((slabs - 1,)),
            pltpu.SemaphoreType.DMA((slabs - 1,)),
        ],
        compiler_params=pltpu.CompilerParams(collective_id=0, has_side_effects=True),
    )(potential_in, charge, cell_kind, coef)

    block = jax.ShapeDtypeStruct((sectors, depth, radial), f32)

    def out_map(g):
        return (jnp.maximum(g - 2, 0), 0, 0)

    return pl.pallas_call(
        drift_body,
        out_shape=(block, block, block),
        grid=(pairs + 2,),
        in_specs=[
            pl.BlockSpec((8, 8, radial), lambda g: (0, 0, 0)),
            pl.BlockSpec((2, 1, tall, radial), lambda g: (0, g, 0, 0)),
            pl.BlockSpec((1, 2, radial), lambda g: (g, 0, 0)),
        ],
        out_specs=(pl.BlockSpec((2, depth, radial), lambda g: (jnp.clip(g - 1, 0, pairs - 1), 0, 0)),)
        + (pl.BlockSpec((2, depth, radial), out_map),) * 2,
        scratch_shapes=[pltpu.VMEM((3, 2, depth, radial), f32)],
    )(coef, field, carry)


def drift_body(coef, field, carry, potential, shift_r, shift_phi, sums):
    step = pl.program_id(0)
    depth, radial = potential.shape[1], potential.shape[2]

    @pl.when(jnp.logical_and(step >= 1, step < pl.num_programs(0) - 1))
    def _():
        mask = parity_mask(radial)
        for at in range(0, depth, 8):
            red = field[0, 0, pl.ds(at + PAD, 8), :]
            black = field[1, 0, pl.ds(at + PAD, 8), :]
            potential[0, pl.ds(at, 8), :] = jnp.where(mask, red, black)
            potential[1, pl.ds(at, 8), :] = jnp.where(mask, black, red)

    drift_kernel(coef, field, carry, potential, shift_r, shift_phi, sums)


def solution(mesh):
    spec = P("phi", "gz", None)
    body = functools.partial(local, mesh.shape["gz"], mesh.shape["phi"])
    return jax.shard_map(body, mesh=mesh, in_specs=(spec,) * 3, out_specs=(spec,) * 3, check_vma=False)
```
